32 devices in a mesh: groups: 2 (over y), row: 4 (over z), col: 2 (over x), mode: 2 (over core).
Axes of the slice: x: 2, y: 2, z: 4, core: 2. Of those that a mesh axis runs over, the one named last changes fastest.
Arguments:
- object_field: float32 [2, 1024, 256], P(None, ('groups', 'row'), 'col'), parts along dimension 1, may hold values from -6 to 6
- probe_modes: float32 [2, 2, 256, 256], P('mode'), may hold values from -1.5 to 1.5
- measured: bfloat16 [8, 2, 2, 256, 256], P(('groups', 'row'), 'col'), parts along dimension 0, may hold values from 0.049804688 to 2
- offset_rows: int32 [8, 2, 2], P(('groups', 'row'), 'col'), parts along dimension 0, may hold values from -128 to -1
- offset_cols: int32 [8, 2, 2], P(('groups', 'row'), 'col'), parts along dimension 0, may hold values from -128 to -1
- pattern_counts: int32 [8, 2], P(('groups', 'row'), 'col'), parts along dimension 0, may hold values from 0 to 2, as said below
Outputs:
- object_out: float32 [2, 1024, 256], P(None, ('groups', 'row'), 'col'), parts along dimension 1
The draws below stay inside these ranges and needn't reach their ends.
There are 2 independent parts, one for each index of `groups`. The reference program is written for one: setup_inputs(seed, part) draws one part's arguments, and reference() takes and returns one part's arrays. A program takes and returns all parts, laid end to end along the dimension named above; an argument that names none is the same for every part. Nothing has to cross between parts.
Inputs may be any that keep to these rules, and one draw needn't show every extreme that they name: `pattern_counts`: slots at or beyond a tile's count are unused; some tile owns exactly 2 patterns.
All inputs are finite; a program needn't handle non-finite values.
Results may differ from the reference program's by a relative error of at most 0.0003.
Values sent between devices are 32-bit elements; how exact they have to be, the bound alone decides.
A program may use at most 64 MiB of HBM per device.

```python
import math
import jax
import jax.numpy as jnp
from jax import lax

P_SIZE = 256
MODES = 2
TR = 128
TC = 128
CAP = 2
ITERS = 2
HALF = 128
ROWT = 4
COLT = 2
NR = 512
NC = 256


def draw_pattern_counts(key, part):
    base = jax.random.randint(jax.random.fold_in(key, 11), (ROWT, COLT), 0, CAP + 1)
    spot_row = jax.random.randint(jax.random.fold_in(key, 12), (), 0, ROWT)
    spot_col = jax.random.randint(jax.random.fold_in(key, 13), (), 0, COLT)
    return base.at[spot_row, spot_col].set(CAP).astype(jnp.int32)


def place_ends(drawn, stream_key, smallest, top_value):
    longest = drawn.shape.index(max(drawn.shape))
    spots = []
    for shift in (0, 1):
        where = [jax.random.randint(jax.random.fold_in(stream_key, axis), (), 0, length) for axis, length in enumerate(drawn.shape)]
        where[longest] = (where[longest] + shift) % drawn.shape[longest]
        spots.append(tuple(where))
    return drawn.at[spots[0]].set(smallest).at[spots[1]].set(top_value)


def shard_levels(rng, extent, shards, low, high):
    factor_of, own = 1.0, jax.random.fold_in(rng, 6)
    for axis_at, blocks in shards:
        heights = jnp.exp(jax.random.uniform(jax.random.fold_in(own, axis_at), (blocks,), jnp.float32, low / len(shards), high / len(shards)))
        factor_of = factor_of * jnp.repeat(heights, extent[axis_at] // blocks).reshape([-1 if axis == axis_at else 1 for axis in range(len(extent))])
    return factor_of


def normal_values(stream_key, extent, width, bound, cuts=(), held_as=jnp.bfloat16):
    loudness = shard_levels(stream_key, extent, cuts, -0.22, 0.18) if cuts else 1.0
    array = jax.random.normal(stream_key, extent, jnp.float32) * width * loudness
    return jnp.minimum(jnp.maximum(array, -bound), bound).astype(held_as)


def setup_inputs(seed: int = 0, part: int = 0) -> dict:
    key_list = jax.random.split(jax.random.key(seed), 7)
    own_keys = jax.random.split(jax.random.fold_in(key_list[6], part), 7)
    return {
        "object_field": normal_values(own_keys[0], (2, NR, NC), 1.0, 6.0, ((1, 4), (2, 2)), jnp.float32),
        "probe_modes": normal_values(key_list[1], (MODES, 2, P_SIZE, P_SIZE), 0.25, 1.5, ((0, 2),), jnp.float32),
        "measured": jnp.clip(jnp.exp(math.log(2.0) - 3.6927934 * jax.random.uniform(own_keys[2], (ROWT, COLT, CAP, P_SIZE, P_SIZE), jnp.float32) ** shard_levels(own_keys[2], (ROWT, COLT, CAP, P_SIZE, P_SIZE), ((0, 4), (1, 2)), -0.2, 0.2)), 0.049804688, 2.0).astype(jnp.bfloat16),
        "offset_rows": place_ends(jax.random.randint(own_keys[3], (ROWT, COLT, CAP), 0 - P_SIZE // 2, TR - P_SIZE // 2), jax.random.fold_in(own_keys[3], 1), 0 - P_SIZE // 2, (TR - P_SIZE // 2) - 1).astype(jnp.int32),
        "offset_cols": place_ends(jax.random.randint(own_keys[4], (ROWT, COLT, CAP), 0 - P_SIZE // 2, TC - P_SIZE // 2), jax.random.fold_in(own_keys[4], 1), 0 - P_SIZE // 2, (TC - P_SIZE // 2) - 1).astype(jnp.int32),
        "pattern_counts": draw_pattern_counts(jax.random.fold_in(jax.random.fold_in(key_list[6], part), 71), part),
    }


step_size = 2.0


def reference(object_field, probe_modes, measured, offset_rows, offset_cols, pattern_counts):
    probe_field = probe_modes[:, 0] + 1j * probe_modes[:, 1]
    tile_row = jnp.repeat(jnp.arange(ROWT, dtype=jnp.int32), COLT * CAP)
    tile_col = jnp.tile(jnp.repeat(jnp.arange(COLT, dtype=jnp.int32), CAP), ROWT)
    slot_index = jnp.tile(jnp.arange(CAP, dtype=jnp.int32), ROWT * COLT)
    row_start = (tile_row * TR + HALF + offset_rows.reshape(-1).astype(jnp.int32)).astype(jnp.int32)
    col_start = (tile_col * TC + HALF + offset_cols.reshape(-1).astype(jnp.int32)).astype(jnp.int32)
    owned_count = pattern_counts.reshape(-1).astype(jnp.int32)[tile_row * COLT + tile_col]
    active = (slot_index < owned_count).astype(jnp.float32)
    observed = measured.reshape(-1, P_SIZE, P_SIZE)
    zero_index = jnp.zeros((), jnp.int32)
    estimate = object_field
    for iteration in range(ITERS):
        padded = jnp.pad(estimate, ((0, 0), (HALF, HALF), (HALF, HALF)))

        def one_pattern(gradient, pattern_data, padded=padded):
            row_at, col_at, weight, target = pattern_data
            window = lax.dynamic_slice(padded, (zero_index, row_at, col_at), (2, P_SIZE, P_SIZE))
            exit_wave = probe_field * (window[0] + 1j * window[1])[None]
            wave = jnp.fft.fft2(exit_wave, norm="ortho")
            intensity = jnp.sum(wave.real * wave.real + wave.imag * wave.imag, axis=0)
            residual = weight * (intensity - target.astype(jnp.float32))
            backward = jnp.fft.ifft2(residual[None] * wave, norm="ortho")
            update = jnp.sum(jnp.conj(probe_field) * backward, axis=0)
            part_grad = jnp.stack([update.real, update.imag])
            current = lax.dynamic_slice(gradient, (zero_index, row_at, col_at), (2, P_SIZE, P_SIZE))
            return lax.dynamic_update_slice(gradient, current + part_grad, (zero_index, row_at, col_at)), None

        gradient, unused = lax.scan(one_pattern, jnp.zeros_like(padded), (row_start, col_start, active, observed))
        estimate = estimate - step_size * gradient[:, HALF:HALF + NR, HALF:HALF + NC]
    return estimate
```

```python
import functools

import jax
import jax.numpy as jnp
import numpy as np
from jax import lax
from jax.experimental import pallas as pl
from jax.experimental.pallas import tpu as pltpu
from jax.sharding import PartitionSpec as P

ITERS = 2
STEP = 2.0
MESH = pl.DeviceIdType.MESH
DIRECTIONS = [(i, j) for i in (-1, 0, 1) for j in (-1, 0, 1) if (i, j) != (0, 0)]


def dft_tables(side):
    index = np.arange(side)
    angles = (index[:, None] * index[None, :] % side) * (2.0 * np.pi / side)
    tables = []
    for table in (np.cos(angles), np.sin(angles)):
        table = (table / np.sqrt(side)).astype(np.float32)
        high = table.astype(jnp.bfloat16)
        low = (table - high.astype(np.float32)).astype(jnp.bfloat16)
        tables += [high, low]
    return np.stack(tables)


def split(x):
    high = x.astype(jnp.bfloat16)
    return high, (x - high.astype(jnp.float32)).astype(jnp.bfloat16)


def dot(a, b):
    return jnp.dot(a, b, preferred_element_type=jnp.float32)


def dot3(a, b):
    return dot(a[0], b[0]) + (dot(a[0], b[1]) + dot(a[1], b[0]))


def kernel(rows_ref, cols_ref, counts_ref, field_ref, probe_ref, measured_ref, table_ref, out_ref,
           ext, grad, partner_grad, received, probe_other, lefts, rights,
           halo_send, halo_recv, fwd_send, fwd_recv, fold_send, fold_recv, own_send, own_recv):
    side = probe_ref.shape[-1]
    half = field_ref.shape[-1]
    n_row, n_col = lax.axis_size("row"), lax.axis_size("col")
    r, c, m = lax.axis_index("row"), lax.axis_index("col"), lax.axis_index("mode")
    other = 1 - m
    partner = {"mode": other}

    def exists(dr, dc):
        return (r + dr >= 0) & (r + dr < n_row) & (c + dc >= 0) & (c + dc < n_col)

    def block(ref, plane, i, j):
        return ref.at[plane, pl.ds(half * (1 + i), half), pl.ds(half * (1 + j), half)]

    for k, (dr, dc) in enumerate(DIRECTIONS):
        @pl.when(jnp.logical_not(exists(-dr, -dc)))
        def _():
            zeros = jnp.zeros((half, half), jnp.float32)
            received[k] = zeros
            for plane in range(2):
                ext[plane, half * (1 - dr):half * (2 - dr), half * (1 - dc):half * (2 - dc)] = zeros
    ext[0, half:2 * half, half:2 * half] = field_ref[0]
    ext[1, half:2 * half, half:2 * half] = field_ref[1]

    barrier = pltpu.get_barrier_semaphore()
    pl.semaphore_signal(barrier, inc=1, device_id=partner, device_id_type=MESH)
    count = 1
    for dr, dc in DIRECTIONS:
        here = exists(dr, dc)
        count = count + here.astype(jnp.int32)

        @pl.when(here)
        def _():
            pl.semaphore_signal(barrier, inc=1, device_id={"row": r + dr, "col": c + dc}, device_id_type=MESH)
    pl.semaphore_wait(barrier, count)

    def remote(src, dst, send, recv, device):
        return pltpu.make_async_remote_copy(
            src_ref=src, dst_ref=dst, send_sem=send, recv_sem=recv, device_id=device, device_id_type=MESH)

    def halo_copy(k):
        dr, dc = DIRECTIONS[k]
        return remote(block(ext, m, 0, 0), block(ext, m, -dr, -dc), halo_send.at[k], halo_recv.at[k],
                      {"row": r + dr, "col": c + dc})

    def forward_copy(k):
        dr, dc = DIRECTIONS[k]
        return remote(block(ext, m, -dr, -dc), block(ext, m, -dr, -dc), fwd_send.at[k], fwd_recv.at[k], partner)

    def fold_copy(k):
        dr, dc = DIRECTIONS[k]
        return remote(block(grad, m, dr, dc), received.at[k], fold_send.at[k], fold_recv.at[k],
                      {"row": r + dr, "col": c + dc})

    probe_copy = remote(probe_ref.at[0], probe_other, own_send.at[0], own_recv.at[0], partner)
    grad_copy = remote(grad.at[other], partner_grad, own_send.at[1], own_recv.at[1], partner)
    center_copy = remote(block(ext, m, 0, 0), block(ext, m, 0, 0), own_send.at[2], own_recv.at[2], partner)

    def start_halo():
        for k, (dr, dc) in enumerate(DIRECTIONS):
            @pl.when(exists(dr, dc))
            def _():
                halo_copy(k).start()

    def finish_halo():
        for k, (dr, dc) in enumerate(DIRECTIONS):
            @pl.when(exists(-dr, -dc))
            def _():
                halo_copy(k).wait_recv()
                forward_copy(k).start()
        for k, (dr, dc) in enumerate(DIRECTIONS):
            @pl.when(exists(-dr, -dc))
            def _():
                forward_copy(k).wait()

            @pl.when(exists(dr, dc))
            def _():
                halo_copy(k).wait_send()

    start_halo()
    probe_copy.start()
    for part in range(2):
        cosine, sine = table_ref[part], table_ref[2 + part]
        rights[part, :side, :side] = cosine
        rights[part, :side, side:] = -sine
        rights[part, side:, :side] = sine
        rights[part, side:, side:] = cosine
        lefts[part, :side, :side] = cosine
        lefts[part, :side, side:] = sine
        lefts[part, side:, :side] = -sine
        lefts[part, side:, side:] = cosine
    row_at = rows_ref[m] + half
    col_at = cols_ref[m] + half
    live = (m < counts_ref[0]).astype(jnp.float32)
    probe_copy.wait()
    width = 3 * half
    row_back, col_back = lax.rem(width - row_at, width), lax.rem(width - col_at, width)

    def swap_in(x):
        top = jnp.concatenate([x[:side, :side], x[side:, :side]], axis=1)
        return jnp.concatenate([top, jnp.concatenate([x[:side, side:], x[side:, side:]], axis=1)], axis=0)

    def iteration(step, carry):
        finish_halo()
        window = [
            pltpu.roll(pltpu.roll(ext[plane], row_back, axis=0)[:side], col_back, axis=1)[:, :side]
            for plane in range(2)
        ]
        probes = [(probe_ref[0, 0], probe_ref[0, 1]), (probe_other[0], probe_other[1])]
        real = [pr * window[0] - pi * window[1] for pr, pi in probes]
        imag = [pr * window[1] + pi * window[0] for pr, pi in probes]
        exit_wave = jnp.concatenate([jnp.concatenate(real, axis=1), jnp.concatenate(imag, axis=1)], axis=0)
        left, right = (lefts[0], lefts[1]), (rights[0], rights[1])
        middle = swap_in(dot3(left, split(exit_wave)))
        wave = dot3(split(middle), right)
        square = wave * wave
        intensity = square[:side, :side] + square[:side, side:] + square[side:, :side] + square[side:, side:]
        residual = live * (intensity - measured_ref[m].astype(jnp.float32))
        residual = jnp.concatenate([residual, residual], axis=1)
        back = wave * jnp.concatenate([residual, residual], axis=0)
        back = swap_in(dot3(split(back), left))
        back = dot3(right, split(back))
        g = [jnp.zeros((side, side), jnp.float32)] * 2
        for q, (pr, pi) in enumerate(probes):
            br = back[:side, side * q:side * (q + 1)]
            bi = back[side:, side * q:side * (q + 1)]
            g = [g[0] + (pr * br + pi * bi), g[1] + (pr * bi - pi * br)]
        for plane in range(2):
            wide = jnp.concatenate([g[plane], jnp.zeros((side, half), jnp.float32)], axis=1)
            wide = pltpu.roll(wide, col_at, axis=1)
            wide = jnp.concatenate([wide, jnp.zeros((half, width), jnp.float32)], axis=0)
            grad[plane] = pltpu.roll(wide, row_at, axis=0)
        grad_copy.start()
        grad_copy.wait()
        grad[m] = grad[m] + partner_grad[...]
        for k, (dr, dc) in enumerate(DIRECTIONS):
            @pl.when(exists(dr, dc))
            def _():
                fold_copy(k).start()
        for k, (dr, dc) in enumerate(DIRECTIONS):
            @pl.when(exists(-dr, -dc))
            def _():
                fold_copy(k).wait_recv()
        total = grad[m, half:2 * half, half:2 * half]
        for k in range(len(DIRECTIONS)):
            total = total + received[k]
        ext[m, half:2 * half, half:2 * half] = ext[m, half:2 * half, half:2 * half] - STEP * total

        @pl.when(step < ITERS - 1)
        def _():
            start_halo()
        center_copy.start()
        for k, (dr, dc) in enumerate(DIRECTIONS):
            @pl.when(exists(dr, dc))
            def _():
                fold_copy(k).wait_send()
        center_copy.wait()
        return carry

    lax.fori_loop(0, ITERS, iteration, 0)
    out_ref[0] = ext[0, half:2 * half, half:2 * half]
    out_ref[1] = ext[1, half:2 * half, half:2 * half]


def body(object_field, probe_modes, measured, offset_rows, offset_cols, pattern_counts):
    side = probe_modes.shape[-1]
    half = object_field.shape[-1]
    width = 3 * half
    smem = pl.BlockSpec(memory_space=pltpu.SMEM)
    vmem = pl.BlockSpec(memory_space=pltpu.VMEM)
    ways = len(DIRECTIONS)
    dma = pltpu.SemaphoreType.DMA
    return pl.pallas_call(
        kernel,
        out_shape=jax.ShapeDtypeStruct(object_field.shape, jnp.float32),
        in_specs=[smem] * 3 + [vmem] * 4,
        out_specs=vmem,
        scratch_shapes=[
            pltpu.VMEM((2, width, width), jnp.float32),
            pltpu.VMEM((2, width, width), jnp.float32),
            pltpu.VMEM((width, width), jnp.float32),
            pltpu.VMEM((ways, half, half), jnp.float32),
            pltpu.VMEM((2, side, side), jnp.float32),
            pltpu.VMEM((2, 2 * side, 2 * side), jnp.bfloat16),
            pltpu.VMEM((2, 2 * side, 2 * side), jnp.bfloat16),
            dma((ways,)), dma((ways,)), dma((ways,)), dma((ways,)), dma((ways,)), dma((ways,)),
            dma((3,)), dma((3,)),
        ],
        compiler_params=pltpu.CompilerParams(
            collective_id=0, has_side_effects=True, vmem_limit_bytes=56 * 1024 * 1024),
    )(offset_rows[0, 0], offset_cols[0, 0], pattern_counts[0], object_field, probe_modes, measured[0, 0],
      jnp.asarray(dft_tables(side)))


def solution(mesh):
    in_specs = (
        P(None, ("groups", "row"), "col"),
        P("mode", None, None, None),
        P(("groups", "row"), "col", None, None, None),
        P(("groups", "row"), "col", None),
        P(("groups", "row"), "col", None),
        P(("groups", "row"), "col"),
    )
    out_specs = P(None, ("groups", "row"), "col")
    return jax.shard_map(body, mesh=mesh, in_specs=in_specs, out_specs=out_specs, check_vma=False)
```

```python
import functools

import jax
import jax.numpy as jnp
import numpy as np
from jax import lax
from jax.experimental import pallas as pl
from jax.experimental.pallas import tpu as pltpu
from jax.sharding import PartitionSpec as P

ITERS = 2
STEP = 2.0
MESH = pl.DeviceIdType.MESH
DIRECTIONS = [(i, j) for i in (-1, 0, 1) for j in (-1, 0, 1) if (i, j) != (0, 0)]


def dft_tables(side):
    index = np.arange(side // 2)
    tables = []
    for parity in range(2):
        angles = ((2 * index[:, None] + parity) * index[None, :] % side) * (2.0 * np.pi / side)
        cosine, sine = np.cos(angles) / np.sqrt(side), np.sin(angles) / np.sqrt(side)
        table = np.block([[cosine, sine], [-sine, cosine]]).astype(np.float32)
        for form in (table, table.T):
            high = form.astype(jnp.bfloat16)
            tables += [high, (form - high.astype(np.float32)).astype(jnp.bfloat16)]
    return np.stack(tables)


def split(x):
    high = x.astype(jnp.bfloat16)
    return high, (x - high.astype(jnp.float32)).astype(jnp.bfloat16)


def dot(a, b):
    return jnp.dot(a, b, preferred_element_type=jnp.float32)


def dot3(a, b):
    return dot(a[0], b[0]) + (dot(a[0], b[1]) + dot(a[1], b[0]))


def kernel(rows_ref, cols_ref, counts_ref, field_ref, probe_ref, measured_ref, table_ref, out_ref,
           ext, grad, raw, partner_raw, received, probe_other, target,
           halo_send, halo_recv, fwd_send, fwd_recv, fold_send, fold_recv, own_send, own_recv):
    side = probe_ref.shape[-1]
    half = field_ref.shape[-1]
    n_row, n_col = lax.axis_size("row"), lax.axis_size("col")
    r, c, m = lax.axis_index("row"), lax.axis_index("col"), lax.axis_index("mode")
    other = 1 - m
    partner = {"mode": other}

    def exists(dr, dc):
        return (r + dr >= 0) & (r + dr < n_row) & (c + dc >= 0) & (c + dc < n_col)

    def block(ref, plane, i, j):
        return ref.at[plane, pl.ds(half * (1 + i), half), pl.ds(half * (1 + j), half)]

    for k, (dr, dc) in enumerate(DIRECTIONS):
        @pl.when(jnp.logical_not(exists(-dr, -dc)))
        def _():
            zeros = jnp.zeros((half, half), jnp.float32)
            received[k] = zeros
            for plane in range(2):
                ext[plane, half * (1 - dr):half * (2 - dr), half * (1 - dc):half * (2 - dc)] = zeros
    ext[0, half:2 * half, half:2 * half] = field_ref[0]
    ext[1, half:2 * half, half:2 * half] = field_ref[1]

    barrier = pltpu.get_barrier_semaphore()
    pl.semaphore_signal(barrier, inc=1, device_id=partner, device_id_type=MESH)
    count = 1
    for dr, dc in DIRECTIONS:
        here = exists(dr, dc)
        count = count + here.astype(jnp.int32)

        @pl.when(here)
        def _():
            pl.semaphore_signal(barrier, inc=1, device_id={"row": r + dr, "col": c + dc}, device_id_type=MESH)
    pl.semaphore_wait(barrier, count)

    def remote(src, dst, send, recv, device):
        return pltpu.make_async_remote_copy(
            src_ref=src, dst_ref=dst, send_sem=send, recv_sem=recv, device_id=device, device_id_type=MESH)

    def halo_copy(k):
        dr, dc = DIRECTIONS[k]
        return remote(block(ext, m, 0, 0), block(ext, m, -dr, -dc), halo_send.at[k], halo_recv.at[k],
                      {"row": r + dr, "col": c + dc})

    def forward_copy(k):
        dr, dc = DIRECTIONS[k]
        return remote(block(ext, m, -dr, -dc), block(ext, m, -dr, -dc), fwd_send.at[k], fwd_recv.at[k], partner)

    def fold_copy(k):
        dr, dc = DIRECTIONS[k]
        return remote(block(grad, m, dr, dc), received.at[k], fold_send.at[k], fold_recv.at[k],
                      {"row": r + dr, "col": c + dc})

    probe_copy = remote(probe_ref.at[0], probe_other, own_send.at[0], own_recv.at[0], partner)
    grad_copy = remote(raw.at[other], partner_raw, own_send.at[1], own_recv.at[1], partner)
    center_copy = remote(block(ext, m, 0, 0), block(ext, m, 0, 0), own_send.at[2], own_recv.at[2], partner)

    def start_halo():
        for k, (dr, dc) in enumerate(DIRECTIONS):
            @pl.when(exists(dr, dc))
            def _():
                halo_copy(k).start()

    def finish_halo():
        for k, (dr, dc) in enumerate(DIRECTIONS):
            @pl.when(exists(-dr, -dc))
            def _():
                halo_copy(k).wait_recv()
                forward_copy(k).start()
        for k, (dr, dc) in enumerate(DIRECTIONS):
            @pl.when(exists(-dr, -dc))
            def _():
                forward_copy(k).wait()

            @pl.when(exists(dr, dc))
            def _():
                halo_copy(k).wait_send()

    start_halo()
    probe_copy.start()
    lines = lax.broadcasted_iota(jnp.int32, (side, side), 0)
    lanes = lax.broadcasted_iota(jnp.int32, (side, side), 1)

    def sorted_by_parity(along, across):
        return (along == jnp.where(across < half, 2 * across, 2 * (across - half) + 1)).astype(
            jnp.float32).astype(jnp.bfloat16)

    target[...] = dot(dot(sorted_by_parity(lanes, lines), measured_ref[m]).astype(jnp.bfloat16),
                      sorted_by_parity(lines, lanes))
    row_at = rows_ref[m] + half
    col_at = cols_ref[m] + half
    live = (m < counts_ref[0]).astype(jnp.float32)
    probe_copy.wait()
    width = 3 * half
    row_back, col_back = lax.rem(width - row_at, width), lax.rem(width - col_at, width)

    def place(g, row, col):
        wide = pltpu.roll(jnp.concatenate([g, jnp.zeros((side, half), jnp.float32)], axis=1), col, axis=1)
        return pltpu.roll(jnp.concatenate([wide, jnp.zeros((half, width), jnp.float32)], axis=0), row, axis=0)

    def halves(x, axis):
        first = lax.slice_in_dim(x, 0, half, axis=axis)
        last = lax.slice_in_dim(x, half, side, axis=axis)
        return first + last, first - last

    def iteration(step, carry):
        finish_halo()
        window = [
            pltpu.roll(pltpu.roll(ext[plane], row_back, axis=0)[:side], col_back, axis=1)[:, :side]
            for plane in range(2)
        ]
        probes = [(probe_ref[0, 0], probe_ref[0, 1]), (probe_other[0], probe_other[1])]
        real = [pr * window[0] - pi * window[1] for pr, pi in probes]
        imag = [pr * window[1] + pi * window[0] for pr, pi in probes]
        real, imag = jnp.concatenate(real, axis=1), jnp.concatenate(imag, axis=1)
        table = [[(table_ref[4 * p + 2 * t], table_ref[4 * p + 2 * t + 1]) for t in range(2)] for p in range(2)]
        real, imag = halves(real, 0), halves(imag, 0)
        middle = [
            dot3(table[p][0], split(jnp.concatenate([real[p], imag[p]], axis=0))) for p in range(2)
        ]
        stacked = [[], []]
        for p in range(2):
            for q in range(2):
                part = middle[p][:, side * q:side * (q + 1)]
                mixed = halves(part, 1)
                for t in range(2):
                    stacked[t].append(jnp.concatenate([mixed[t][:half], mixed[t][half:]], axis=1))
        wave = [dot3(split(jnp.concatenate(stacked[t], axis=0)), table[t][1]) for t in range(2)]
        back = []
        for t in range(2):
            square = wave[t] * wave[t]
            square = square[:, :half] + square[:, half:]
            parts = []
            for p in range(2):
                intensity = square[side * p:side * p + half] + square[side * p + half:side * (p + 1)]
                residual = live * (intensity - target[half * p:half * (p + 1), half * t:half * (t + 1)])
                residual = jnp.concatenate([residual, residual], axis=1)
                parts += [residual, residual]
            back.append(dot3(split(wave[t] * jnp.concatenate(parts, axis=0)), table[t][0]))
        both = (back[0] + back[1], back[0] - back[1])
        last = []
        for p in range(2):
            sides = []
            for plane in range(2):
                sides.append(jnp.concatenate(
                    [both[t][side * p + half * q:side * p + half * (q + 1), half * plane:half * (plane + 1)]
                     for q in range(2) for t in range(2)], axis=1))
            last.append(dot3(table[p][1], split(jnp.concatenate(sides, axis=0))))
        both = (last[0] + last[1], last[0] - last[1])
        g = [jnp.zeros((side, side), jnp.float32)] * 2
        for q, (pr, pi) in enumerate(probes):
            br, bi = [
                jnp.concatenate([part[half * plane:half * (plane + 1), side * q:side * (q + 1)] for part in both], axis=0)
                for plane in range(2)
            ]
            g = [g[0] + (pr * br + pi * bi), g[1] + (pr * bi - pi * br)]
        raw[0] = g[0]
        raw[1] = g[1]
        grad_copy.start()
        own = place(raw[m], row_at, col_at)
        grad_copy.wait()
        grad[m] = own + place(partner_raw[...], rows_ref[other] + half, cols_ref[other] + half)
        for k, (dr, dc) in enumerate(DIRECTIONS):
            @pl.when(exists(dr, dc))
            def _():
                fold_copy(k).start()
        for k, (dr, dc) in enumerate(DIRECTIONS):
            @pl.when(exists(-dr, -dc))
            def _():
                fold_copy(k).wait_recv()
        total = grad[m, half:2 * half, half:2 * half]
        for k in range(len(DIRECTIONS)):
            total = total + received[k]
        ext[m, half:2 * half, half:2 * half] = ext[m, half:2 * half, half:2 * half] - STEP * total

        @pl.when(step < ITERS - 1)
        def _():
            start_halo()
        center_copy.start()
        for k, (dr, dc) in enumerate(DIRECTIONS):
            @pl.when(exists(dr, dc))
            def _():
                fold_copy(k).wait_send()
        center_copy.wait()
        return carry

    lax.fori_loop(0, ITERS, iteration, 0)
    out_ref[0] = ext[0, half:2 * half, half:2 * half]
    out_ref[1] = ext[1, half:2 * half, half:2 * half]


def body(object_field, probe_modes, measured, offset_rows, offset_cols, pattern_counts):
    side = probe_modes.shape[-1]
    half = object_field.shape[-1]
    width = 3 * half
    smem = pl.BlockSpec(memory_space=pltpu.SMEM)
    vmem = pl.BlockSpec(memory_space=pltpu.VMEM)
    ways = len(DIRECTIONS)
    dma = pltpu.SemaphoreType.DMA
    return pl.pallas_call(
        kernel,
        out_shape=jax.ShapeDtypeStruct(object_field.shape, jnp.float32),
        in_specs=[smem] * 3 + [vmem] * 4,
        out_specs=vmem,
        scratch_shapes=[
            pltpu.VMEM((2, width, width), jnp.float32),
            pltpu.VMEM((2, width, width), jnp.float32),
            pltpu.VMEM((2, side, side), jnp.float32),
            pltpu.VMEM((side, side), jnp.float32),
            pltpu.VMEM((ways, half, half), jnp.float32),
            pltpu.VMEM((2, side, side), jnp.float32),
            pltpu.VMEM((side, side), jnp.float32),
            dma((ways,)), dma((ways,)), dma((ways,)), dma((ways,)), dma((ways,)), dma((ways,)),
            dma((3,)), dma((3,)),
        ],
        compiler_params=pltpu.CompilerParams(
            collective_id=0, has_side_effects=True, vmem_limit_bytes=56 * 1024 * 1024),
    )(offset_rows[0, 0], offset_cols[0, 0], pattern_counts[0], object_field, probe_modes, measured[0, 0],
      jnp.asarray(dft_tables(side)))


def solution(mesh):
    in_specs = (
        P(None, ("groups", "row"), "col"),
        P("mode", None, None, None),
        P(("groups", "row"), "col", None, None, None),
        P(("groups", "row"), "col", None),
        P(("groups", "row"), "col", None),
        P(("groups", "row"), "col"),
    )
    out_specs = P(None, ("groups", "row"), "col")
    return jax.shard_map(body, mesh=mesh, in_specs=in_specs, out_specs=out_specs, check_vma=False)
```
